32 devices in a mesh: alpha: 4 (over y, core), beta: 8 (over z, x).
Axes of the slice: x: 2, y: 2, z: 4, core: 2. Of those that a mesh axis runs over, the one named last changes fastest.
Arguments:
- coeffs: float32 [8, 1024], P('alpha', 'beta'), may hold values from -6 to 6
- alpha_target: int32 [8, 132], P('alpha'), may hold values from 0 to 7
- alpha_pair: int32 [8, 132], P('alpha'), may hold values from 0 to 483
- alpha_sign: int32 [8, 132], P('alpha'), may hold values from -1 to 1
- beta_target: int32 [1024, 132], P('beta'), may hold values from 0 to 1023
- beta_pair: int32 [1024, 132], P('beta'), may hold values from 0 to 483
- beta_sign: int32 [1024, 132], P('beta'), may hold values from -1 to 1
- integrals: float32 [484, 484], replicated
- one_body: float32 [22, 22], replicated
Outputs:
- sigma: float32 [8, 1024], P('alpha', 'beta')
The draws below stay inside these ranges and needn't reach their ends.
All inputs are finite; a program needn't handle non-finite values.
Results may differ from the reference program's by a relative error of at most 0.0003.
Values sent between devices are 32-bit elements; how exact they have to be, the bound alone decides.
A program may use at most 64 MiB of HBM per device.

```python
import jax
import jax.numpy as jnp
from jax import lax

NORB = 22
SLOTS = 132
ROWB = 1
PAIRS = 484
NA = 8
NB = 1024


def draw_integrals(key, part):
    shape = (NORB, NORB, NORB, NORB)
    base = jax.random.normal(key, shape, jnp.float32)
    sym = base + jnp.transpose(base, (1, 0, 2, 3))
    sym = sym + jnp.transpose(sym, (0, 1, 3, 2))
    sym = sym + jnp.transpose(sym, (2, 3, 0, 1))
    return (sym * (2.8284271 / 8.0 / SLOTS)).reshape(NORB * NORB, NORB * NORB)


def draw_one_body(key, part):
    base = jax.random.normal(key, (NORB, NORB), jnp.float32)
    return (base + base.T) * (0.05 / 1.4142136)


def touch_ends(entries, own_key, smallest, high):
    longest = entries.shape.index(max(entries.shape))
    spots = []
    for shift in (0, 1):
        where = [jax.random.randint(jax.random.fold_in(own_key, axis), (), 0, length) for axis, length in enumerate(entries.shape)]
        where[longest] = (where[longest] + shift) % entries.shape[longest]
        spots.append(tuple(where))
    return entries.at[spots[0]].set(smallest).at[spots[1]].set(high)


def level_of(own_key, dims, cuts, smallest, largest):
    loudness = 1.0
    for position, parts in cuts:
        heights = jax.random.uniform(jax.random.fold_in(jax.random.fold_in(own_key, 6), position), (parts,), jnp.float32, smallest / len(cuts), largest / len(cuts))
        loudness = loudness * jnp.repeat(jnp.exp(heights), dims[position] // parts).reshape((-1,) + (1,) * (len(dims) - 1 - position))
    return loudness


def bell_draw(rng, extent, scale, reach, pieces=(), kind=jnp.bfloat16):
    loudness = level_of(rng, extent, pieces, -0.22, 0.18) if pieces else 1.0
    values = jax.random.normal(rng, extent, jnp.float32) * scale * loudness
    return jnp.minimum(jnp.maximum(values, -reach), reach).astype(kind)


def setup_inputs(seed: int = 0) -> dict:
    key_list = jax.random.split(jax.random.key(seed), 10)
    return {
        "coeffs": bell_draw(key_list[0], (NA, NB), 1.0, 6.0, ((0, 4), (1, 8)), jnp.float32),
        "alpha_target": touch_ends(jax.random.randint(key_list[1], (NA, SLOTS), 0, NA), jax.random.fold_in(key_list[1], 1), 0, NA - 1).astype(jnp.int32),
        "alpha_pair": touch_ends(jax.random.randint(key_list[2], (NA, SLOTS), 0, PAIRS), jax.random.fold_in(key_list[2], 1), 0, PAIRS - 1).astype(jnp.int32),
        "alpha_sign": touch_ends(jax.random.randint(key_list[3], (NA, SLOTS), -1, 2), jax.random.fold_in(key_list[3], 1), -1, 1).astype(jnp.int32),
        "beta_target": touch_ends(jax.random.randint(key_list[4], (NB, SLOTS), 0, NB), jax.random.fold_in(key_list[4], 1), 0, NB - 1).astype(jnp.int32),
        "beta_pair": touch_ends(jax.random.randint(key_list[5], (NB, SLOTS), 0, PAIRS), jax.random.fold_in(key_list[5], 1), 0, PAIRS - 1).astype(jnp.int32),
        "beta_sign": touch_ends(jax.random.randint(key_list[6], (NB, SLOTS), -1, 2), jax.random.fold_in(key_list[6], 1), -1, 1).astype(jnp.int32),
        "integrals": draw_integrals(jax.random.fold_in(key_list[9], 71), 0),
        "one_body": draw_one_body(jax.random.fold_in(key_list[9], 71), 0),
    }


def reference(coeffs, alpha_target, alpha_pair, alpha_sign, beta_target, beta_pair, beta_sign, integrals, one_body):
    highest = lax.Precision.HIGHEST
    h_flat = one_body.reshape(PAIRS)
    pair_ids = jnp.arange(PAIRS, dtype=jnp.int32)
    swapped = ((beta_pair % NORB) * NORB + beta_pair // NORB).astype(jnp.int32)
    beta_cols = jnp.arange(NB, dtype=jnp.int32)[:, None]
    beta_phase = beta_sign.astype(jnp.float32)
    flat_target = beta_target.reshape(NB * SLOTS)

    def one_block(inputs):
        targets, pairs, signs, c_rows = inputs
        gathered = coeffs[targets]
        picks = (pairs[:, :, None] == pair_ids[None, None, :]).astype(jnp.float32) * signs.astype(jnp.float32)[:, :, None]
        dens = jnp.einsum("isp,isb->ipb", picks, gathered, precision=highest)
        fock = jnp.einsum("pq,ipb->iqb", integrals, dens, precision=highest) + h_flat[None, :, None] * c_rows[:, None, :]
        local = jnp.einsum("p,ipb->ib", h_flat, dens, precision=highest)
        values = fock[:, swapped, beta_cols] * beta_phase[None, :, :]
        spread = jax.ops.segment_sum(values.reshape(ROWB, NB * SLOTS).T, flat_target, num_segments=NB)
        return local + spread.T

    blocks = NA // ROWB
    result = lax.map(one_block, (alpha_target.reshape(blocks, ROWB, SLOTS), alpha_pair.reshape(blocks, ROWB, SLOTS), alpha_sign.reshape(blocks, ROWB, SLOTS), coeffs.reshape(blocks, ROWB, NB)))
    return result.reshape(NA, NB)
```

```python
import functools

import jax
import jax.numpy as jnp
from jax import lax
from jax.experimental import pallas as pl
from jax.experimental.pallas import tpu as pltpu
from jax.sharding import PartitionSpec as P

MESH = pl.DeviceIdType.MESH
LANES = 128
NT = (((1,), (1,)), ((), ()))
NN = (((1,), (0,)), ((), ()))


def dot(a, b, dims=NN):
    return lax.dot_general(a, b, dims, preferred_element_type=jnp.float32)


def split(x):
    top = x.astype(jnp.bfloat16).astype(jnp.float32)
    return top, x - top


def divider(n, limit):
    s = 16
    m = (1 << s) // n + 1
    assert all((x * m) >> s == x // n for x in range(limit)) and limit * m < 2**31
    return m, s


def lane_pick(table, lane, chunk):
    out = None
    for i in range(table.shape[1] // LANES):
        part = jnp.take_along_axis(
            table[:, i * LANES : (i + 1) * LANES], lane, axis=1, mode="promise_in_bounds"
        )
        out = part if out is None else jnp.where(chunk == i, part, out)
    return out


def kernel(
    na,
    nb,
    step_rows,
    coeffs,
    a_target,
    a_pair,
    a_sign,
    b_target,
    b_pair,
    b_sign,
    integrals,
    one_body,
    out,
    at_v,
    ap_v,
    as_v,
    bt_v,
    bp_v,
    bs_v,
    int_v,
    ob_v,
    slab,
    g_v,
    owner_v,
    lo_v,
    vals,
    hot,
    send,
    recv,
    load_sem,
    ag_send,
    ag_recv,
    rs_send,
    rs_recv,
):
    rows, cols = coeffs.shape
    slots = a_target.shape[1]
    norb = one_body.shape[0]
    npairs = norb * norb
    wide = g_v.shape[1]
    alphas = na * rows
    me_a = lax.axis_index("alpha")
    me_b = lax.axis_index("beta")
    f32, bf16 = jnp.float32, jnp.bfloat16

    loads = [
        pltpu.make_async_copy(src, dst, load_sem.at[i])
        for i, (src, dst) in enumerate(
            (
                (a_target, at_v),
                (a_pair, ap_v),
                (a_sign, as_v),
                (one_body, ob_v),
                (integrals, int_v),
                (b_target, bt_v),
                (b_pair, bp_v),
                (b_sign, bs_v),
            )
        )
    ]
    for load in loads:
        load.start()
    barrier = pltpu.get_barrier_semaphore()
    for k in range(1, na):
        pl.semaphore_signal(barrier, inc=1, device_id=(lax.rem(me_a + k, na), me_b), device_id_type=MESH)
    for k in range(1, nb):
        pl.semaphore_signal(barrier, inc=1, device_id=(me_a, lax.rem(me_b + k, nb)), device_id_type=MESH)
    pl.semaphore_wait(barrier, na + nb - 2)

    gathers = []
    for k in range(1, na):
        copy = pltpu.make_async_remote_copy(
            src_ref=coeffs,
            dst_ref=slab.at[me_a],
            send_sem=ag_send.at[k],
            recv_sem=ag_recv.at[k],
            device_id=(lax.rem(me_a + k, na), me_b),
            device_id_type=MESH,
        )
        copy.start()
        gathers.append(copy)

    for i in range(5):
        loads[i].wait()
    pair_ids = lax.broadcasted_iota(jnp.int32, (wide, slots), 0)
    string_ids = lax.broadcasted_iota(jnp.int32, (alphas, slots), 0)
    counts = []
    for a in range(rows):
        hits = jnp.where(pair_ids == ap_v[a : a + 1, :], 1.0, 0.0).astype(bf16)
        reach = jnp.where(string_ids == at_v[a : a + 1, :], as_v[a : a + 1, :].astype(f32), 0.0)
        counts.append(dot(reach.astype(bf16), hits, NT))
    counts = jnp.concatenate(counts, axis=0)
    mul, shift = divider(norb, wide)
    q = lax.broadcasted_iota(jnp.int32, (norb, wide), 1)
    q_row = (q * mul) >> shift
    q_col = q - q_row * norb
    orbital = lax.broadcasted_iota(jnp.int32, (norb, wide), 0)
    spread_h = lax.dot_general(
        ob_v[...],
        jnp.where(q_col == orbital, 1.0, 0.0),
        NN,
        precision=lax.Precision.HIGHEST,
        preferred_element_type=f32,
    )
    h = jnp.sum(jnp.where(q_row == orbital, spread_h, 0.0), axis=0, keepdims=True)
    weight = jnp.sum(counts * h, axis=1, keepdims=True)
    exact = counts[:, :npairs].astype(bf16)
    int_top, int_rest = split(int_v[...])
    g_v[...] = jnp.zeros_like(g_v)
    g_v[:, :npairs] = dot(exact, int_top.astype(bf16)) + dot(exact, int_rest.astype(bf16))
    line = lax.broadcasted_iota(jnp.int32, (rows * alphas, wide), 0)
    own = line == me_a * rows
    for a in range(1, rows):
        own = own | (line == a * alphas + me_a * rows + a)
    g = g_v[...] + jnp.where(own, h, 0.0)

    full, rem = slots // LANES, slots % LANES
    loads[5].wait()
    bits = cols.bit_length() - 1

    def to_rows(ref, values):
        for i in range(full):
            ref[i * cols : (i + 1) * cols, :] = values[i]
        if rem:
            ref[full * cols : full * cols + rem, :] = values[full].T[:rem, :]

    def chunks(ref):
        parts = [ref[:, i * LANES : (i + 1) * LANES] for i in range(full)]
        if rem:
            last = ref[:, full * LANES :]
            parts.append(jnp.concatenate([last, jnp.zeros((cols, LANES - rem), last.dtype)], axis=1))
        return parts

    targets = [t.astype(f32) for t in chunks(bt_v)]
    targets = [jnp.floor(t * (1.0 / cols)) for t in targets], targets
    to_rows(owner_v, targets[0])
    to_rows(lo_v, [t - o * cols for o, t in zip(*targets)])
    lo_ids = lax.broadcasted_iota(jnp.int32, (cols, LANES), 0).astype(f32)
    items = slots * cols // LANES

    @pl.loop(0, items // step_rows)
    def _(i):
        for r in range(step_rows):
            row = i * step_rows + r
            match = lo_ids == lo_v[pl.ds(row, 1), :]
            hot[:, pl.ds(pl.multiple_of(row * LANES, LANES), LANES)] = jnp.where(match, 1.0, 0.0).astype(bf16)

    loads[6].wait()
    loads[7].wait()
    lanes, pieces, signs = [], [], []
    for p, s in zip(chunks(bp_v), chunks(bs_v)):
        k = (p * mul) >> shift
        swapped = (p - k * norb) * norb + k
        lanes.append(swapped & (LANES - 1))
        pieces.append(swapped >> (LANES.bit_length() - 1))
        signs.append(s.astype(f32))

    for copy in gathers:
        copy.wait()
    slab[me_a] = coeffs[...]
    c = jnp.concatenate([slab[i] for i in range(na)], axis=0)
    c_top, c_rest = split(c)
    lhs = jnp.concatenate([c_top, c_rest, c_top], axis=0).T.astype(bf16)
    local = []
    for a in range(rows):
        local.append(jnp.sum(weight[a * alphas : (a + 1) * alphas] * c, axis=0, keepdims=True))
        g_top, g_rest = split(g[a * alphas : (a + 1) * alphas])
        fock = dot(lhs, jnp.concatenate([g_top, g_top, g_rest], axis=0).astype(bf16))
        picked = [lane_pick(fock, l, p) * s for l, p, s in zip(lanes, pieces, signs)]
        parts = [split(v) for v in picked]
        to_rows(vals.at[a], [v[0] for v in parts])
        to_rows(vals.at[rows + a], [v[1] for v in parts])

    owner_ids = lax.broadcasted_iota(jnp.int32, (nb, LANES), 0).astype(f32)

    def step(i, total):
        lhs = []
        for r in range(step_rows):
            row = i * step_rows + r
            match = owner_ids == owner_v[pl.ds(row, 1), :]
            lhs.append(
                jnp.concatenate([jnp.where(match, vals[m, pl.ds(row, 1), :], 0.0) for m in range(2 * rows)], axis=0)
            )
        lhs = jnp.concatenate(lhs, axis=1).astype(bf16)
        width = step_rows * LANES
        return total + dot(lhs, hot[:, pl.ds(pl.multiple_of(i * width, LANES), width)], NT)

    total = lax.fori_loop(0, items // step_rows, step, jnp.zeros((2 * rows * nb, cols), f32))
    for a in range(rows):
        send[:, a, :] = total[a * nb : (a + 1) * nb] + total[(rows + a) * nb : (rows + a + 1) * nb]

    copies = []
    for k in range(1, nb):
        to = lax.rem(me_b + k, nb)
        copy = pltpu.make_async_remote_copy(
            src_ref=send.at[to],
            dst_ref=recv.at[k],
            send_sem=rs_send.at[k],
            recv_sem=rs_recv.at[k],
            device_id=(me_a, to),
            device_id_type=MESH,
        )
        copy.start()
        copies.append(copy)
    result = jnp.concatenate(local, axis=0) + send[me_b]
    for copy in copies:
        copy.wait()
    for k in range(1, nb):
        result = result + recv[k]
    out[...] = result


def solution(mesh):
    na, nb = mesh.shape["alpha"], mesh.shape["beta"]

    def per_device(coeffs, a_target, a_pair, a_sign, b_target, b_pair, b_sign, integrals, one_body):
        rows, cols = coeffs.shape
        slots = a_target.shape[1]
        norb = one_body.shape[0]
        wide = pl.cdiv(norb * norb, LANES) * LANES
        items = slots * cols // LANES
        step_rows = next(n for n in (6, 4, 3, 2, 1) if items % n == 0)
        i32, f32 = jnp.int32, jnp.float32
        padded = pl.cdiv(items, 8) * 8
        return pl.pallas_call(
            functools.partial(kernel, na, nb, step_rows),
            out_shape=jax.ShapeDtypeStruct((rows, cols), f32),
            in_specs=[pl.BlockSpec(memory_space=pltpu.VMEM)] + [pl.BlockSpec(memory_space=pl.ANY)] * 8,
            out_specs=pl.BlockSpec(memory_space=pltpu.VMEM),
            scratch_shapes=[
                pltpu.VMEM(a_target.shape, i32),
                pltpu.VMEM(a_pair.shape, i32),
                pltpu.VMEM(a_sign.shape, i32),
                pltpu.VMEM(b_target.shape, i32),
                pltpu.VMEM(b_pair.shape, i32),
                pltpu.VMEM(b_sign.shape, i32),
                pltpu.VMEM(integrals.shape, f32),
                pltpu.VMEM(one_body.shape, f32),
                pltpu.VMEM((na, rows, cols), f32),
                pltpu.VMEM((rows * na * rows, wide), f32),
                pltpu.VMEM((padded, LANES), f32),
                pltpu.VMEM((padded, LANES), f32),
                pltpu.VMEM((2 * rows, padded, LANES), f32),
                pltpu.VMEM((cols, items * LANES), jnp.bfloat16),
                pltpu.VMEM((nb, rows, cols), f32),
                pltpu.VMEM((nb, rows, cols), f32),
                pltpu.SemaphoreType.DMA((8,)),
                pltpu.SemaphoreType.DMA((na,)),
                pltpu.SemaphoreType.DMA((na,)),
                pltpu.SemaphoreType.DMA((nb,)),
                pltpu.SemaphoreType.DMA((nb,)),
            ],
            compiler_params=pltpu.CompilerParams(collective_id=0, has_side_effects=True),
        )(coeffs, a_target, a_pair, a_sign, b_target, b_pair, b_sign, integrals, one_body)

    placed = (
        P("alpha", "beta"),
        P("alpha", None),
        P("alpha", None),
        P("alpha", None),
        P("beta", None),
        P("beta", None),
        P("beta", None),
        P(),
        P(),
    )
    return jax.shard_map(
        per_device, mesh=mesh, in_specs=placed, out_specs=P("alpha", "beta"), check_vma=False
    )
```

```python
import functools

import jax
import jax.numpy as jnp
from jax import lax
from jax.experimental import pallas as pl
from jax.experimental.pallas import tpu as pltpu
from jax.sharding import PartitionSpec as P

MESH = pl.DeviceIdType.MESH
LANES = 128
NT = (((1,), (1,)), ((), ()))
NN = (((1,), (0,)), ((), ()))


def dot(a, b, dims=NN):
    return lax.dot_general(a, b, dims, preferred_element_type=jnp.float32)


def split(x):
    top = x.astype(jnp.bfloat16).astype(jnp.float32)
    return top, x - top


def divider(n, limit):
    s = 16
    m = (1 << s) // n + 1
    assert all((x * m) >> s == x // n for x in range(limit)) and limit * m < 2**31
    return m, s


def lane_pick(table, lane, chunk):
    out = None
    for i in range(table.shape[1] // LANES):
        part = jnp.take_along_axis(
            table[:, i * LANES : (i + 1) * LANES], lane, axis=1, mode="promise_in_bounds"
        )
        out = part if out is None else jnp.where(chunk == i, part, out)
    return out


def kernel(
    na,
    nb,
    build_rows,
    step_rows,
    coeffs,
    a_target,
    a_pair,
    a_sign,
    b_target,
    b_pair,
    b_sign,
    integrals,
    one_body,
    out,
    c_v,
    at_v,
    ap_v,
    as_v,
    bt_v,
    bp_v,
    bs_v,
    int_v,
    ob_v,
    slab,
    g_v,
    owner_v,
    lo_v,
    vals,
    hot,
    send,
    recv,
    load_sem,
    ag_send,
    ag_recv,
    rs_send,
    rs_recv,
):
    rows, cols = coeffs.shape
    slots = a_target.shape[1]
    norb = one_body.shape[0]
    npairs = norb * norb
    wide = g_v.shape[1]
    alphas = na * rows
    me_a = lax.axis_index("alpha")
    me_b = lax.axis_index("beta")
    f32, bf16 = jnp.float32, jnp.bfloat16

    loads = [
        pltpu.make_async_copy(src, dst, load_sem.at[i])
        for i, (src, dst) in enumerate(
            (
                (coeffs, c_v),
                (a_target, at_v),
                (a_pair, ap_v),
                (a_sign, as_v),
                (one_body, ob_v),
                (integrals, int_v),
                (b_target, bt_v),
                (b_pair, bp_v),
                (b_sign, bs_v),
            )
        )
    ]
    for load in loads:
        load.start()
    barrier = pltpu.get_barrier_semaphore()
    for k in range(1, na):
        pl.semaphore_signal(barrier, inc=1, device_id=(lax.rem(me_a + k, na), me_b), device_id_type=MESH)
    for k in range(1, nb):
        pl.semaphore_signal(barrier, inc=1, device_id=(me_a, lax.rem(me_b + k, nb)), device_id_type=MESH)
    for i in range(1, 6):
        loads[i].wait()
    pair_ids = lax.broadcasted_iota(jnp.int32, (wide, slots), 0)
    string_ids = lax.broadcasted_iota(jnp.int32, (alphas, slots), 0)
    counts = []
    for a in range(rows):
        hits = jnp.where(pair_ids == ap_v[a : a + 1, :], 1.0, 0.0).astype(bf16)
        reach = jnp.where(string_ids == at_v[a : a + 1, :], as_v[a : a + 1, :].astype(f32), 0.0)
        counts.append(dot(reach.astype(bf16), hits, NT))
    counts = jnp.concatenate(counts, axis=0)
    mul, shift = divider(norb, wide)
    q = lax.broadcasted_iota(jnp.int32, (norb, wide), 1)
    q_row = (q * mul) >> shift
    q_col = q - q_row * norb
    orbital = lax.broadcasted_iota(jnp.int32, (norb, wide), 0)
    spread_h = lax.dot_general(
        ob_v[...],
        jnp.where(q_col == orbital, 1.0, 0.0),
        NN,
        precision=lax.Precision.HIGHEST,
        preferred_element_type=f32,
    )
    h = jnp.sum(jnp.where(q_row == orbital, spread_h, 0.0), axis=0, keepdims=True)
    weight = jnp.sum(counts * h, axis=1, keepdims=True)
    exact = counts[:, :npairs].astype(bf16)
    int_top, int_rest = split(int_v[...])
    g_v[...] = jnp.zeros_like(g_v)
    g_v[:, :npairs] = dot(exact, int_top.astype(bf16)) + dot(exact, int_rest.astype(bf16))
    line = lax.broadcasted_iota(jnp.int32, (rows * alphas, wide), 0)
    own = line == me_a * rows
    for a in range(1, rows):
        own = own | (line == a * alphas + me_a * rows + a)
    g = g_v[...] + jnp.where(own, h, 0.0)

    full, rem = slots // LANES, slots % LANES
    for i in range(6, 9):
        loads[i].wait()
    pair_bits = (wide - 1).bit_length()
    column_bits = (cols - 1).bit_length()

    def swap(pair):
        row = (pair * mul) >> shift
        return (pair - row * norb) * norb + row

    def pack(lower, upper):
        swapped = swap(bp_v[lower:upper, :])
        return (bt_v[lower:upper, :] << (pair_bits + 2)) | (swapped << 2) | (bs_v[lower:upper, :] + 1)

    codes = [pack(i * LANES, (i + 1) * LANES).astype(f32).T.astype(jnp.int32) for i in range(full)]
    for i, code in enumerate(codes):
        target = code >> (pair_bits + 2)
        owner_v[i * cols : (i + 1) * cols, :] = (target >> column_bits).astype(f32)
        lo_v[i * cols : (i + 1) * cols, :] = (target & (cols - 1)).astype(f32)
    if rem:
        target = bt_v[full * LANES :, :]
        owner_v[full * cols : full * cols + rem, :] = (target >> column_bits).astype(f32)
        lo_v[full * cols : full * cols + rem, :] = (target & (cols - 1)).astype(f32)
        tail = pack(full * LANES, slots).astype(f32)
        tail = jnp.concatenate([tail] * rows + [jnp.zeros((LANES - rows * rem, cols), f32)], axis=0)
        codes.append(tail.T.astype(jnp.int32))
    swapped = [(code >> 2) & ((1 << pair_bits) - 1) for code in codes]
    signs = [((code & 3) - 1).astype(f32) for code in codes]
    lanes = [index & (LANES - 1) for index in swapped]
    pieces = [index >> (LANES.bit_length() - 1) for index in swapped]

    loads[0].wait()
    pl.semaphore_wait(barrier, na + nb - 2)

    gathers = []
    for k in range(1, na):
        copy = pltpu.make_async_remote_copy(
            src_ref=c_v,
            dst_ref=slab.at[me_a],
            send_sem=ag_send.at[k - 1],
            recv_sem=ag_recv.at[k - 1],
            device_id=(lax.rem(me_a + k, na), me_b),
            device_id_type=MESH,
        )
        copy.start()
        gathers.append(copy)

    lo_ids = lax.broadcasted_iota(jnp.int32, (cols, LANES), 0).astype(f32).astype(bf16)
    items = slots * cols // LANES

    @pl.loop(0, items // build_rows)
    def _(i):
        for r in range(build_rows):
            row = i * build_rows + r
            wanted = jnp.broadcast_to(lo_v[pl.ds(row, 1), :].astype(bf16), (cols, LANES))
            match = jnp.where(lo_ids == wanted, jnp.ones((), bf16), jnp.zeros((), bf16))
            hot[:, pl.ds(pl.multiple_of(row * LANES, LANES), LANES)] = match

    for copy in gathers:
        copy.wait()
    slab[me_a] = c_v[...]
    c = jnp.concatenate([slab[i] for i in range(na)], axis=0)
    c_top, c_rest = split(c)
    lhs = jnp.concatenate([c_top, c_rest, c_top], axis=0).T.astype(bf16)
    local, focks = [], []
    for a in range(rows):
        local.append(jnp.sum(weight[a * alphas : (a + 1) * alphas] * c, axis=0, keepdims=True))
        g_top, g_rest = split(g[a * alphas : (a + 1) * alphas])
        focks.append(dot(lhs, jnp.concatenate([g_top, g_top, g_rest], axis=0).astype(bf16)))
    for i in range(full):
        for a in range(rows):
            top, rest = split(lane_pick(focks[a], lanes[i], pieces[i]) * signs[i])
            vals[a, i * cols : (i + 1) * cols, :] = top
            vals[rows + a, i * cols : (i + 1) * cols, :] = rest
    if rem:
        lane_ids = lax.broadcasted_iota(jnp.int32, (cols, LANES), 1)
        tail = lane_pick(focks[0], lanes[full], pieces[full])
        for a in range(1, rows):
            tail = jnp.where(lane_ids < a * rem, tail, lane_pick(focks[a], lanes[full], pieces[full]))
        top, rest = split((tail * signs[full]).T)
        for a in range(rows):
            vals[a, full * cols : full * cols + rem, :] = top[a * rem : (a + 1) * rem]
            vals[rows + a, full * cols : full * cols + rem, :] = rest[a * rem : (a + 1) * rem]

    owner_ids = lax.broadcasted_iota(jnp.int32, (nb, LANES), 0).astype(f32)

    def step(i, total):
        lhs = []
        for r in range(step_rows):
            row = i * step_rows + r
            match = owner_ids == owner_v[pl.ds(row, 1), :]
            lhs.append(
                jnp.concatenate([jnp.where(match, vals[m, pl.ds(row, 1), :], 0.0) for m in range(2 * rows)], axis=0)
            )
        lhs = jnp.concatenate(lhs, axis=1).astype(bf16)
        width = step_rows * LANES
        return total + dot(lhs, hot[:, pl.ds(pl.multiple_of(i * width, LANES), width)], NT)

    total = lax.fori_loop(0, items // step_rows, step, jnp.zeros((2 * rows * nb, cols), f32))
    for a in range(rows):
        send[:, a, :] = total[a * nb : (a + 1) * nb] + total[(rows + a) * nb : (rows + a + 1) * nb]

    copies = []
    for k in range(1, nb):
        to = lax.rem(me_b + k, nb)
        copy = pltpu.make_async_remote_copy(
            src_ref=send.at[to],
            dst_ref=recv.at[k - 1],
            send_sem=rs_send.at[k - 1],
            recv_sem=rs_recv.at[k - 1],
            device_id=(me_a, to),
            device_id_type=MESH,
        )
        copy.start()
        copies.append(copy)
    result = jnp.concatenate(local, axis=0) + send[me_b]
    for copy in copies:
        copy.wait()
    for k in range(1, nb):
        result = result + recv[k - 1]
    out[...] = result


def solution(mesh):
    na, nb = mesh.shape["alpha"], mesh.shape["beta"]

    def per_device(coeffs, a_target, a_pair, a_sign, b_target, b_pair, b_sign, integrals, one_body):
        rows, cols = coeffs.shape
        slots = a_target.shape[1]
        norb = one_body.shape[0]
        wide = pl.cdiv(norb * norb, LANES) * LANES
        items = slots * cols // LANES
        build_rows = next(n for n in range(12, 0, -1) if items % n == 0)
        step_rows = next(n for n in range(24, 0, -1) if items % n == 0)
        i32, f32 = jnp.int32, jnp.float32
        padded = pl.cdiv(items, 8) * 8
        return pl.pallas_call(
            functools.partial(kernel, na, nb, build_rows, step_rows),
            out_shape=jax.ShapeDtypeStruct((rows, cols), f32),
            in_specs=[pl.BlockSpec(memory_space=pl.ANY)] * 9,
            out_specs=pl.BlockSpec(memory_space=pltpu.VMEM),
            scratch_shapes=[
                pltpu.VMEM(coeffs.shape, f32),
                pltpu.VMEM(a_target.shape, i32),
                pltpu.VMEM(a_pair.shape, i32),
                pltpu.VMEM(a_sign.shape, i32),
                pltpu.VMEM(b_target.shape[::-1], i32),
                pltpu.VMEM(b_pair.shape[::-1], i32),
                pltpu.VMEM(b_sign.shape[::-1], i32),
                pltpu.VMEM(integrals.shape, f32),
                pltpu.VMEM(one_body.shape, f32),
                pltpu.VMEM((na, rows, cols), f32),
                pltpu.VMEM((rows * na * rows, wide), f32),
                pltpu.VMEM((padded, LANES), f32),
                pltpu.VMEM((padded, LANES), f32),
                pltpu.VMEM((2 * rows, padded, LANES), f32),
                pltpu.VMEM((cols, items * LANES), jnp.bfloat16),
                pltpu.VMEM((nb, rows, cols), f32),
                pltpu.VMEM((nb - 1, rows, cols), f32),
                pltpu.SemaphoreType.DMA((9,)),
                pltpu.SemaphoreType.DMA((na - 1,)),
                pltpu.SemaphoreType.DMA((na - 1,)),
                pltpu.SemaphoreType.DMA((nb - 1,)),
                pltpu.SemaphoreType.DMA((nb - 1,)),
            ],
            compiler_params=pltpu.CompilerParams(collective_id=0, has_side_effects=True),
        )(coeffs, a_target, a_pair, a_sign, b_target.T, b_pair.T, b_sign.T, integrals, one_body)

    placed = (
        P("alpha", "beta"),
        P("alpha", None),
        P("alpha", None),
        P("alpha", None),
        P("beta", None),
        P("beta", None),
        P("beta", None),
        P(),
        P(),
    )
    return jax.shard_map(
        per_device, mesh=mesh, in_specs=placed, out_specs=P("alpha", "beta"), check_vma=False
    )
```

```python
import functools

import jax
import jax.numpy as jnp
from jax import lax
from jax.experimental import pallas as pl
from jax.experimental.pallas import tpu as pltpu
from jax.sharding import PartitionSpec as P

MESH = pl.DeviceIdType.MESH
LANES = 128
NT = (((1,), (1,)), ((), ()))
NN = (((1,), (0,)), ((), ()))


def dot(a, b, dims=NN):
    return lax.dot_general(a, b, dims, preferred_element_type=jnp.float32)


def split(x):
    top = x.astype(jnp.bfloat16).astype(jnp.float32)
    return top, x - top


def divider(n, limit):
    s = 16
    m = (1 << s) // n + 1
    assert all((x * m) >> s == x // n for x in range(limit)) and limit * m < 2**31
    return m, s


def lane_pick(table, lane, chunk):
    out = None
    for i in range(table.shape[1] // LANES):
        part = jnp.take_along_axis(
            table[:, i * LANES : (i + 1) * LANES], lane, axis=1, mode="promise_in_bounds"
        )
        out = part if out is None else jnp.where(chunk == i, part, out)
    return out


def kernel(
    na,
    nb,
    build_rows,
    step_rows,
    coeffs,
    a_target,
    a_pair,
    a_sign,
    b_target,
    b_pair,
    b_sign,
    integrals,
    one_body,
    out,
    c_v,
    at_v,
    ap_v,
    as_v,
    bt_v,
    bp_v,
    bs_v,
    int_v,
    ob_v,
    slab,
    g_v,
    owner_v,
    lo_v,
    vals,
    hot,
    send,
    recv,
    load_sem,
    ag_send,
    ag_recv,
    rs_send,
    rs_recv,
):
    rows, cols = coeffs.shape
    slots = a_target.shape[1]
    norb = one_body.shape[0]
    npairs = norb * norb
    wide = g_v.shape[1]
    alphas = na * rows
    me_a = lax.axis_index("alpha")
    me_b = lax.axis_index("beta")
    f32, bf16 = jnp.float32, jnp.bfloat16

    loads = [
        pltpu.make_async_copy(src, dst, load_sem.at[i])
        for i, (src, dst) in enumerate(
            (
                (coeffs, c_v),
                (a_target, at_v),
                (a_pair, ap_v),
                (a_sign, as_v),
                (one_body, ob_v),
                (integrals, int_v),
                (b_target, bt_v),
                (b_pair, bp_v),
                (b_sign, bs_v),
            )
        )
    ]
    for load in loads:
        load.start()
    barrier = pltpu.get_barrier_semaphore()
    for k in range(1, na):
        pl.semaphore_signal(barrier, inc=1, device_id=(lax.rem(me_a + k, na), me_b), device_id_type=MESH)
    for k in range(1, nb):
        pl.semaphore_signal(barrier, inc=1, device_id=(me_a, lax.rem(me_b + k, nb)), device_id_type=MESH)
    loads[0].wait()
    pl.semaphore_wait(barrier, na + nb - 2)

    gathers = []
    for k in range(1, na):
        copy = pltpu.make_async_remote_copy(
            src_ref=c_v,
            dst_ref=slab.at[me_a],
            send_sem=ag_send.at[k - 1],
            recv_sem=ag_recv.at[k - 1],
            device_id=(lax.rem(me_a + k, na), me_b),
            device_id_type=MESH,
        )
        copy.start()
        gathers.append(copy)

    for i in range(1, 6):
        loads[i].wait()
    pair_ids = lax.broadcasted_iota(jnp.int32, (wide, slots), 0)
    string_ids = lax.broadcasted_iota(jnp.int32, (alphas, slots), 0)
    counts = []
    for a in range(rows):
        hits = jnp.where(pair_ids == ap_v[a : a + 1, :], 1.0, 0.0).astype(bf16)
        reach = jnp.where(string_ids == at_v[a : a + 1, :], as_v[a : a + 1, :].astype(f32), 0.0)
        counts.append(dot(reach.astype(bf16), hits, NT))
    counts = jnp.concatenate(counts, axis=0)
    mul, shift = divider(norb, wide)
    q = lax.broadcasted_iota(jnp.int32, (norb, wide), 1)
    q_row = (q * mul) >> shift
    q_col = q - q_row * norb
    orbital = lax.broadcasted_iota(jnp.int32, (norb, wide), 0)
    spread_h = lax.dot_general(
        ob_v[...],
        jnp.where(q_col == orbital, 1.0, 0.0),
        NN,
        precision=lax.Precision.HIGHEST,
        preferred_element_type=f32,
    )
    h = jnp.sum(jnp.where(q_row == orbital, spread_h, 0.0), axis=0, keepdims=True)
    weight = jnp.sum(counts * h, axis=1, keepdims=True)
    exact = counts[:, :npairs].astype(bf16)
    int_top, int_rest = split(int_v[...])
    g_v[...] = jnp.zeros_like(g_v)
    g_v[:, :npairs] = dot(exact, int_top.astype(bf16)) + dot(exact, int_rest.astype(bf16))
    line = lax.broadcasted_iota(jnp.int32, (rows * alphas, wide), 0)
    own = line == me_a * rows
    for a in range(1, rows):
        own = own | (line == a * alphas + me_a * rows + a)
    g = g_v[...] + jnp.where(own, h, 0.0)

    full, rem = slots // LANES, slots % LANES
    for i in range(6, 9):
        loads[i].wait()
    pair_bits = (wide - 1).bit_length()
    column_bits = (cols - 1).bit_length()

    def swap(pair):
        row = (pair * mul) >> shift
        return (pair - row * norb) * norb + row

    def pack(lower, upper):
        swapped = swap(bp_v[lower:upper, :])
        return (bt_v[lower:upper, :] << (pair_bits + 2)) | (swapped << 2) | (bs_v[lower:upper, :] + 1)

    codes = [pack(i * LANES, (i + 1) * LANES).astype(f32).T.astype(jnp.int32) for i in range(full)]
    for i, code in enumerate(codes):
        target = code >> (pair_bits + 2)
        owner_v[i * cols : (i + 1) * cols, :] = (target >> column_bits).astype(f32)
        lo_v[i * cols : (i + 1) * cols, :] = (target & (cols - 1)).astype(f32)
    if rem:
        target = bt_v[full * LANES :, :]
        owner_v[full * cols : full * cols + rem, :] = (target >> column_bits).astype(f32)
        lo_v[full * cols : full * cols + rem, :] = (target & (cols - 1)).astype(f32)
        tail = pack(full * LANES, slots).astype(f32)
        tail = jnp.concatenate([tail] * rows + [jnp.zeros((LANES - rows * rem, cols), f32)], axis=0)
        codes.append(tail.T.astype(jnp.int32))
    swapped = [(code >> 2) & ((1 << pair_bits) - 1) for code in codes]
    signs = [((code & 3) - 1).astype(f32) for code in codes]
    lanes = [index & (LANES - 1) for index in swapped]
    pieces = [index >> (LANES.bit_length() - 1) for index in swapped]

    lo_ids = lax.broadcasted_iota(jnp.int32, (cols, LANES), 0).astype(f32).astype(bf16)
    items = slots * cols // LANES

    @pl.loop(0, items // build_rows)
    def _(i):
        for r in range(build_rows):
            row = i * build_rows + r
            wanted = jnp.broadcast_to(lo_v[pl.ds(row, 1), :].astype(bf16), (cols, LANES))
            match = jnp.where(lo_ids == wanted, jnp.ones((), bf16), jnp.zeros((), bf16))
            hot[:, pl.ds(pl.multiple_of(row * LANES, LANES), LANES)] = match

    for copy in gathers:
        copy.wait()
    slab[me_a] = c_v[...]
    c = jnp.concatenate([slab[i] for i in range(na)], axis=0)
    c_top, c_rest = split(c)
    lhs = jnp.concatenate([c_top, c_rest, c_top], axis=0).T.astype(bf16)
    local, focks = [], []
    for a in range(rows):
        local.append(jnp.sum(weight[a * alphas : (a + 1) * alphas] * c, axis=0, keepdims=True))
        g_top, g_rest = split(g[a * alphas : (a + 1) * alphas])
        focks.append(dot(lhs, jnp.concatenate([g_top, g_top, g_rest], axis=0).astype(bf16)))
    for i in range(full):
        for a in range(rows):
            top, rest = split(lane_pick(focks[a], lanes[i], pieces[i]) * signs[i])
            vals[a, i * cols : (i + 1) * cols, :] = top
            vals[rows + a, i * cols : (i + 1) * cols, :] = rest
    if rem:
        lane_ids = lax.broadcasted_iota(jnp.int32, (cols, LANES), 1)
        tail = lane_pick(focks[0], lanes[full], pieces[full])
        for a in range(1, rows):
            tail = jnp.where(lane_ids < a * rem, tail, lane_pick(focks[a], lanes[full], pieces[full]))
        top, rest = split((tail * signs[full]).T)
        for a in range(rows):
            vals[a, full * cols : full * cols + rem, :] = top[a * rem : (a + 1) * rem]
            vals[rows + a, full * cols : full * cols + rem, :] = rest[a * rem : (a + 1) * rem]

    owner_ids = lax.broadcasted_iota(jnp.int32, (nb, LANES), 0).astype(f32)

    def step(i, total):
        lhs = []
        for r in range(step_rows):
            row = i * step_rows + r
            match = owner_ids == owner_v[pl.ds(row, 1), :]
            lhs.append(
                jnp.concatenate([jnp.where(match, vals[m, pl.ds(row, 1), :], 0.0) for m in range(2 * rows)], axis=0)
            )
        lhs = jnp.concatenate(lhs, axis=1).astype(bf16)
        width = step_rows * LANES
        return total + dot(lhs, hot[:, pl.ds(pl.multiple_of(i * width, LANES), width)], NT)

    total = lax.fori_loop(0, items // step_rows, step, jnp.zeros((2 * rows * nb, cols), f32))
    for a in range(rows):
        send[:, a, :] = total[a * nb : (a + 1) * nb] + total[(rows + a) * nb : (rows + a + 1) * nb]

    copies = []
    for k in range(1, nb):
        to = lax.rem(me_b + k, nb)
        copy = pltpu.make_async_remote_copy(
            src_ref=send.at[to],
            dst_ref=recv.at[k - 1],
            send_sem=rs_send.at[k - 1],
            recv_sem=rs_recv.at[k - 1],
            device_id=(me_a, to),
            device_id_type=MESH,
        )
        copy.start()
        copies.append(copy)
    result = jnp.concatenate(local, axis=0) + send[me_b]
    for copy in copies:
        copy.wait()
    for k in range(1, nb):
        result = result + recv[k - 1]
    out[...] = result


def solution(mesh):
    na, nb = mesh.shape["alpha"], mesh.shape["beta"]

    def per_device(coeffs, a_target, a_pair, a_sign, b_target, b_pair, b_sign, integrals, one_body):
        rows, cols = coeffs.shape
        slots = a_target.shape[1]
        norb = one_body.shape[0]
        wide = pl.cdiv(norb * norb, LANES) * LANES
        items = slots * cols // LANES
        build_rows = next(n for n in range(12, 0, -1) if items % n == 0)
        step_rows = next(n for n in range(24, 0, -1) if items % n == 0)
        i32, f32 = jnp.int32, jnp.float32
        padded = pl.cdiv(items, 8) * 8
        return pl.pallas_call(
            functools.partial(kernel, na, nb, build_rows, step_rows),
            out_shape=jax.ShapeDtypeStruct((rows, cols), f32),
            in_specs=[pl.BlockSpec(memory_space=pl.ANY)] * 9,
            out_specs=pl.BlockSpec(memory_space=pltpu.VMEM),
            scratch_shapes=[
                pltpu.VMEM(coeffs.shape, f32),
                pltpu.VMEM(a_target.shape, i32),
                pltpu.VMEM(a_pair.shape, i32),
                pltpu.VMEM(a_sign.shape, i32),
                pltpu.VMEM(b_target.shape[::-1], i32),
                pltpu.VMEM(b_pair.shape[::-1], i32),
                pltpu.VMEM(b_sign.shape[::-1], i32),
                pltpu.VMEM(integrals.shape, f32),
                pltpu.VMEM(one_body.shape, f32),
                pltpu.VMEM((na, rows, cols), f32),
                pltpu.VMEM((rows * na * rows, wide), f32),
                pltpu.VMEM((padded, LANES), f32),
                pltpu.VMEM((padded, LANES), f32),
                pltpu.VMEM((2 * rows, padded, LANES), f32),
                pltpu.VMEM((cols, items * LANES), jnp.bfloat16),
                pltpu.VMEM((nb, rows, cols), f32),
                pltpu.VMEM((nb - 1, rows, cols), f32),
                pltpu.SemaphoreType.DMA((9,)),
                pltpu.SemaphoreType.DMA((na - 1,)),
                pltpu.SemaphoreType.DMA((na - 1,)),
                pltpu.SemaphoreType.DMA((nb - 1,)),
                pltpu.SemaphoreType.DMA((nb - 1,)),
            ],
            compiler_params=pltpu.CompilerParams(collective_id=0, has_side_effects=True),
        )(coeffs, a_target, a_pair, a_sign, b_target.T, b_pair.T, b_sign.T, integrals, one_body)

    placed = (
        P("alpha", "beta"),
        P("alpha", None),
        P("alpha", None),
        P("alpha", None),
        P("beta", None),
        P("beta", None),
        P("beta", None),
        P(),
        P(),
    )
    return jax.shard_map(
        per_device, mesh=mesh, in_specs=placed, out_specs=P("alpha", "beta"), check_vma=False
    )
```

```python
import functools

import jax
import jax.numpy as jnp
from jax import lax
from jax.experimental import pallas as pl
from jax.experimental.pallas import tpu as pltpu
from jax.sharding import PartitionSpec as P

MESH = pl.DeviceIdType.MESH
LANES = 128
NT = (((1,), (1,)), ((), ()))
NN = (((1,), (0,)), ((), ()))


def dot(a, b, dims=NN):
    return lax.dot_general(a, b, dims, preferred_element_type=jnp.float32)


def split(x):
    top = x.astype(jnp.bfloat16).astype(jnp.float32)
    return top, x - top


def divider(n, limit):
    s = 16
    m = (1 << s) // n + 1
    assert all((x * m) >> s == x // n for x in range(limit)) and limit * m < 2**31
    return m, s


def lane_pick(table, lane, chunk):
    out = None
    for i in range(table.shape[1] // LANES):
        part = jnp.take_along_axis(
            table[:, i * LANES : (i + 1) * LANES], lane, axis=1, mode="promise_in_bounds"
        )
        out = part if out is None else jnp.where(chunk == i, part, out)
    return out


def kernel(
    na,
    nb,
    build_rows,
    step_rows,
    coeffs,
    a_target,
    a_pair,
    a_sign,
    b_target,
    b_pair,
    b_sign,
    integrals,
    one_body,
    out,
    c_v,
    at_v,
    ap_v,
    as_v,
    bt_v,
    bp_v,
    bs_v,
    int_v,
    ob_v,
    slab,
    g_v,
    owner_v,
    lo_v,
    vals,
    hot,
    send,
    recv,
    load_sem,
    ag_send,
    ag_recv,
    rs_send,
    rs_recv,
):
    rows, cols = coeffs.shape
    slots = a_target.shape[1]
    norb = one_body.shape[0]
    npairs = norb * norb
    wide = g_v.shape[1]
    alphas = na * rows
    me_a = lax.axis_index("alpha")
    me_b = lax.axis_index("beta")
    f32, bf16 = jnp.float32, jnp.bfloat16

    loads = [
        pltpu.make_async_copy(src, dst, load_sem.at[i])
        for i, (src, dst) in enumerate(
            (
                (coeffs, c_v),
                (a_target, at_v),
                (a_pair, ap_v),
                (a_sign, as_v),
                (one_body, ob_v),
                (integrals, int_v),
                (b_target, bt_v),
                (b_pair, bp_v),
                (b_sign, bs_v),
            )
        )
    ]
    for load in loads:
        load.start()
    barrier = pltpu.get_barrier_semaphore()
    for k in range(1, na):
        pl.semaphore_signal(barrier, inc=1, device_id=(lax.rem(me_a + k, na), me_b), device_id_type=MESH)
    for k in range(1, nb):
        pl.semaphore_signal(barrier, inc=1, device_id=(me_a, lax.rem(me_b + k, nb)), device_id_type=MESH)
    loads[0].wait()
    pl.semaphore_wait(barrier, na + nb - 2)

    gathers = []
    for k in range(1, na):
        copy = pltpu.make_async_remote_copy(
            src_ref=c_v,
            dst_ref=slab.at[me_a],
            send_sem=ag_send.at[k - 1],
            recv_sem=ag_recv.at[k - 1],
            device_id=(lax.rem(me_a + k, na), me_b),
            device_id_type=MESH,
        )
        copy.start()
        gathers.append(copy)

    for i in range(1, 6):
        loads[i].wait()
    pair_ids = lax.broadcasted_iota(jnp.int32, (wide, slots), 0)
    string_ids = lax.broadcasted_iota(jnp.int32, (alphas, slots), 0)
    counts = []
    for a in range(rows):
        hits = jnp.where(pair_ids == ap_v[a : a + 1, :], 1.0, 0.0).astype(bf16)
        reach = jnp.where(string_ids == at_v[a : a + 1, :], as_v[a : a + 1, :].astype(f32), 0.0)
        counts.append(dot(reach.astype(bf16), hits, NT))
    counts = jnp.concatenate(counts, axis=0)
    mul, shift = divider(norb, wide)
    q = lax.broadcasted_iota(jnp.int32, (norb, wide), 1)
    q_row = (q * mul) >> shift
    q_col = q - q_row * norb
    orbital = lax.broadcasted_iota(jnp.int32, (norb, wide), 0)
    spread_h = lax.dot_general(
        ob_v[...],
        jnp.where(q_col == orbital, 1.0, 0.0),
        NN,
        precision=lax.Precision.HIGHEST,
        preferred_element_type=f32,
    )
    h = jnp.sum(jnp.where(q_row == orbital, spread_h, 0.0), axis=0, keepdims=True)
    weight = jnp.sum(counts * h, axis=1, keepdims=True)
    exact = counts[:, :npairs].astype(bf16)
    int_top, int_rest = split(int_v[...])
    g_v[...] = jnp.zeros_like(g_v)
    g_v[:, :npairs] = dot(exact, int_top.astype(bf16)) + dot(exact, int_rest.astype(bf16))
    line = lax.broadcasted_iota(jnp.int32, (rows * alphas, wide), 0)
    own = line == me_a * rows
    for a in range(1, rows):
        own = own | (line == a * alphas + me_a * rows + a)
    g = g_v[...] + jnp.where(own, h, 0.0)

    full, rem = slots // LANES, slots % LANES
    for i in range(6, 9):
        loads[i].wait()
    pair_bits = (wide - 1).bit_length()
    column_bits = (cols - 1).bit_length()

    def swap(pair):
        row = (pair * mul) >> shift
        return (pair - row * norb) * norb + row

    def pack(lower, upper):
        swapped = swap(bp_v[lower:upper, :])
        return (bt_v[lower:upper, :] << (pair_bits + 2)) | (swapped << 2) | (bs_v[lower:upper, :] + 1)

    codes = [pack(i * LANES, (i + 1) * LANES).astype(f32).T.astype(jnp.int32) for i in range(full)]
    for i, code in enumerate(codes):
        target = code >> (pair_bits + 2)
        owner_v[i * cols : (i + 1) * cols, :] = (target >> column_bits).astype(f32)
        lo_v[i * cols : (i + 1) * cols, :] = (target & (cols - 1)).astype(f32)
    if rem:
        target = bt_v[full * LANES :, :]
        owner_v[full * cols : full * cols + rem, :] = (target >> column_bits).astype(f32)
        lo_v[full * cols : full * cols + rem, :] = (target & (cols - 1)).astype(f32)
        tail = pack(full * LANES, slots).astype(f32)
        tail = jnp.concatenate([tail] * rows + [jnp.zeros((LANES - rows * rem, cols), f32)], axis=0)
        codes.append(tail.T.astype(jnp.int32))
    swapped = [(code >> 2) & ((1 << pair_bits) - 1) for code in codes]
    signs = [((code & 3) - 1).astype(f32) for code in codes]
    lanes = [index & (LANES - 1) for index in swapped]
    pieces = [index >> (LANES.bit_length() - 1) for index in swapped]

    lo_ids = lax.broadcasted_iota(jnp.int32, (cols, LANES), 0).astype(f32).astype(bf16)
    items = slots * cols // LANES

    @pl.loop(0, items // build_rows)
    def _(i):
        for r in range(build_rows):
            row = i * build_rows + r
            wanted = jnp.broadcast_to(lo_v[pl.ds(row, 1), :].astype(bf16), (cols, LANES))
            match = jnp.where(lo_ids == wanted, jnp.ones((), bf16), jnp.zeros((), bf16))
            hot[:, pl.ds(pl.multiple_of(row * LANES, LANES), LANES)] = match

    for copy in gathers:
        copy.wait()
    slab[me_a] = c_v[...]
    c = jnp.concatenate([slab[i] for i in range(na)], axis=0)
    c_top, c_rest = split(c)
    lhs = jnp.concatenate([c_top, c_rest, c_top], axis=0).T.astype(bf16)
    local, focks = [], []
    for a in range(rows):
        local.append(jnp.sum(weight[a * alphas : (a + 1) * alphas] * c, axis=0, keepdims=True))
        g_top, g_rest = split(g[a * alphas : (a + 1) * alphas])
        focks.append(dot(lhs, jnp.concatenate([g_top, g_top, g_rest], axis=0).astype(bf16)))
    for i in range(full):
        for a in range(rows):
            top, rest = split(lane_pick(focks[a], lanes[i], pieces[i]) * signs[i])
            vals[a, i * cols : (i + 1) * cols, :] = top
            vals[rows + a, i * cols : (i + 1) * cols, :] = rest
    if rem:
        lane_ids = lax.broadcasted_iota(jnp.int32, (cols, LANES), 1)
        tail = lane_pick(focks[0], lanes[full], pieces[full])
        for a in range(1, rows):
            tail = jnp.where(lane_ids < a * rem, tail, lane_pick(focks[a], lanes[full], pieces[full]))
        top, rest = split((tail * signs[full]).T)
        for a in range(rows):
            vals[a, full * cols : full * cols + rem, :] = top[a * rem : (a + 1) * rem]
            vals[rows + a, full * cols : full * cols + rem, :] = rest[a * rem : (a + 1) * rem]

    owner_ids = lax.broadcasted_iota(jnp.int32, (nb, LANES), 0).astype(f32)

    def step(i, total):
        lhs = []
        for r in range(step_rows):
            row = i * step_rows + r
            match = owner_ids == owner_v[pl.ds(row, 1), :]
            lhs.append(
                jnp.concatenate([jnp.where(match, vals[m, pl.ds(row, 1), :], 0.0) for m in range(2 * rows)], axis=0)
            )
        lhs = jnp.concatenate(lhs, axis=1).astype(bf16)
        width = step_rows * LANES
        return total + dot(hot[:, pl.ds(pl.multiple_of(i * width, LANES), width)], lhs, NT)

    total = lax.fori_loop(0, items // step_rows, step, jnp.zeros((cols, 2 * rows * nb), f32))
    if total.shape[1] % LANES:
        total = jnp.concatenate([total, jnp.zeros((cols, -total.shape[1] % LANES), f32)], axis=1)
    total = total.T
    for a in range(rows):
        send[:, a, :] = total[a * nb : (a + 1) * nb] + total[(rows + a) * nb : (rows + a + 1) * nb]

    copies = []
    for k in range(1, nb):
        to = lax.rem(me_b + k, nb)
        copy = pltpu.make_async_remote_copy(
            src_ref=send.at[to],
            dst_ref=recv.at[k - 1],
            send_sem=rs_send.at[k - 1],
            recv_sem=rs_recv.at[k - 1],
            device_id=(me_a, to),
            device_id_type=MESH,
        )
        copy.start()
        copies.append(copy)
    result = jnp.concatenate(local, axis=0) + send[me_b]
    for copy in copies:
        copy.wait()
    for k in range(1, nb):
        result = result + recv[k - 1]
    out[...] = result


def solution(mesh):
    na, nb = mesh.shape["alpha"], mesh.shape["beta"]

    def per_device(coeffs, a_target, a_pair, a_sign, b_target, b_pair, b_sign, integrals, one_body):
        rows, cols = coeffs.shape
        slots = a_target.shape[1]
        norb = one_body.shape[0]
        wide = pl.cdiv(norb * norb, LANES) * LANES
        items = slots * cols // LANES
        build_rows = next(n for n in range(12, 0, -1) if items % n == 0)
        step_rows = items
        i32, f32 = jnp.int32, jnp.float32
        padded = pl.cdiv(items, 8) * 8
        return pl.pallas_call(
            functools.partial(kernel, na, nb, build_rows, step_rows),
            out_shape=jax.ShapeDtypeStruct((rows, cols), f32),
            in_specs=[pl.BlockSpec(memory_space=pl.ANY)] * 9,
            out_specs=pl.BlockSpec(memory_space=pltpu.VMEM),
            scratch_shapes=[
                pltpu.VMEM(coeffs.shape, f32),
                pltpu.VMEM(a_target.shape, i32),
                pltpu.VMEM(a_pair.shape, i32),
                pltpu.VMEM(a_sign.shape, i32),
                pltpu.VMEM(b_target.shape[::-1], i32),
                pltpu.VMEM(b_pair.shape[::-1], i32),
                pltpu.VMEM(b_sign.shape[::-1], i32),
                pltpu.VMEM(integrals.shape, f32),
                pltpu.VMEM(one_body.shape, f32),
                pltpu.VMEM((na, rows, cols), f32),
                pltpu.VMEM((rows * na * rows, wide), f32),
                pltpu.VMEM((padded, LANES), f32),
                pltpu.VMEM((padded, LANES), f32),
                pltpu.VMEM((2 * rows, padded, LANES), f32),
                pltpu.VMEM((cols, items * LANES), jnp.bfloat16),
                pltpu.VMEM((nb, rows, cols), f32),
                pltpu.VMEM((nb - 1, rows, cols), f32),
                pltpu.SemaphoreType.DMA((9,)),
                pltpu.SemaphoreType.DMA((na - 1,)),
                pltpu.SemaphoreType.DMA((na - 1,)),
                pltpu.SemaphoreType.DMA((nb - 1,)),
                pltpu.SemaphoreType.DMA((nb - 1,)),
            ],
            compiler_params=pltpu.CompilerParams(collective_id=0, has_side_effects=True),
        )(coeffs, a_target, a_pair, a_sign, b_target.T, b_pair.T, b_sign.T, integrals, one_body)

    placed = (
        P("alpha", "beta"),
        P("alpha", None),
        P("alpha", None),
        P("alpha", None),
        P("beta", None),
        P("beta", None),
        P("beta", None),
        P(),
        P(),
    )
    return jax.shard_map(
        per_device, mesh=mesh, in_specs=placed, out_specs=P("alpha", "beta"), check_vma=False
    )
```

```python
import functools

import jax
import jax.numpy as jnp
from jax import lax
from jax.experimental import pallas as pl
from jax.experimental.pallas import tpu as pltpu
from jax.sharding import PartitionSpec as P

MESH = pl.DeviceIdType.MESH
LANES = 128
NT = (((1,), (1,)), ((), ()))
NN = (((1,), (0,)), ((), ()))


def dot(a, b, dims=NN):
    return lax.dot_general(a, b, dims, preferred_element_type=jnp.float32)


def split(x):
    top = x.astype(jnp.bfloat16).astype(jnp.float32)
    return top, x - top


def divider(n, limit):
    s = 16
    m = (1 << s) // n + 1
    assert all((x * m) >> s == x // n for x in range(limit)) and limit * m < 2**31
    return m, s


def lane_pick(table, lane, chunk):
    out = None
    for i in range(table.shape[1] // LANES):
        part = jnp.take_along_axis(
            table[:, i * LANES : (i + 1) * LANES], lane, axis=1, mode="promise_in_bounds"
        )
        out = part if out is None else jnp.where(chunk == i, part, out)
    return out


def kernel(
    na,
    nb,
    build_rows,
    step_rows,
    coeffs,
    a_target,
    a_pair,
    a_sign,
    b_target,
    b_pair,
    b_sign,
    integrals,
    one_body,
    out,
    c_v,
    at_v,
    ap_v,
    as_v,
    bt_v,
    bp_v,
    bs_v,
    int_v,
    ob_v,
    slab,
    g_v,
    owner_v,
    lo_v,
    vals,
    hot,
    send,
    recv,
    load_sem,
    ag_send,
    ag_recv,
    rs_send,
    rs_recv,
):
    rows, cols = coeffs.shape
    slots = a_target.shape[1]
    norb = one_body.shape[0]
    npairs = norb * norb
    wide = g_v.shape[1]
    alphas = na * rows
    me_a = lax.axis_index("alpha")
    me_b = lax.axis_index("beta")
    f32, bf16 = jnp.float32, jnp.bfloat16

    loads = [
        pltpu.make_async_copy(src, dst, load_sem.at[i])
        for i, (src, dst) in enumerate(
            (
                (coeffs, c_v),
                (a_target, at_v),
                (a_pair, ap_v),
                (a_sign, as_v),
                (one_body, ob_v),
                (integrals, int_v),
                (b_target, bt_v),
                (b_pair, bp_v),
                (b_sign, bs_v),
            )
        )
    ]
    for load in loads:
        load.start()
    barrier = pltpu.get_barrier_semaphore()
    for k in range(1, na):
        pl.semaphore_signal(barrier, inc=1, device_id=(lax.rem(me_a + k, na), me_b), device_id_type=MESH)
    for k in range(1, nb):
        pl.semaphore_signal(barrier, inc=1, device_id=(me_a, lax.rem(me_b + k, nb)), device_id_type=MESH)
    loads[0].wait()
    pl.semaphore_wait(barrier, na + nb - 2)

    gathers = []
    for k in range(1, na):
        copy = pltpu.make_async_remote_copy(
            src_ref=c_v,
            dst_ref=slab.at[me_a],
            send_sem=ag_send.at[k - 1],
            recv_sem=ag_recv.at[k - 1],
            device_id=(lax.rem(me_a + k, na), me_b),
            device_id_type=MESH,
        )
        copy.start()
        gathers.append(copy)

    for i in range(1, 6):
        loads[i].wait()
    pair_ids = lax.broadcasted_iota(jnp.int32, (wide, slots), 0)
    string_ids = lax.broadcasted_iota(jnp.int32, (alphas, slots), 0)
    counts = []
    for a in range(rows):
        hits = jnp.where(pair_ids == ap_v[a : a + 1, :], 1.0, 0.0).astype(bf16)
        reach = jnp.where(string_ids == at_v[a : a + 1, :], as_v[a : a + 1, :].astype(f32), 0.0)
        counts.append(dot(reach.astype(bf16), hits, NT))
    counts = jnp.concatenate(counts, axis=0)
    mul, shift = divider(norb, wide)
    q = lax.broadcasted_iota(jnp.int32, (norb, wide), 1)
    q_row = (q * mul) >> shift
    q_col = q - q_row * norb
    orbital = lax.broadcasted_iota(jnp.int32, (norb, wide), 0)
    spread_h = lax.dot_general(
        ob_v[...],
        jnp.where(q_col == orbital, 1.0, 0.0),
        NN,
        precision=lax.Precision.HIGHEST,
        preferred_element_type=f32,
    )
    h = jnp.sum(jnp.where(q_row == orbital, spread_h, 0.0), axis=0, keepdims=True)
    weight = jnp.sum(counts * h, axis=1, keepdims=True)
    exact = counts[:, :npairs].astype(bf16)
    int_top, int_rest = split(int_v[...])
    g_v[...] = jnp.zeros_like(g_v)
    g_v[:, :npairs] = dot(exact, int_top.astype(bf16)) + dot(exact, int_rest.astype(bf16))
    line = lax.broadcasted_iota(jnp.int32, (rows * alphas, wide), 0)
    own = line == me_a * rows
    for a in range(1, rows):
        own = own | (line == a * alphas + me_a * rows + a)
    g = g_v[...] + jnp.where(own, h, 0.0)

    full, rem = slots // LANES, slots % LANES
    for i in range(6, 9):
        loads[i].wait()
    pair_bits = (wide - 1).bit_length()
    column_bits = (cols - 1).bit_length()

    def swap(pair):
        row = (pair * mul) >> shift
        return (pair - row * norb) * norb + row

    def pack(lower, upper):
        swapped = swap(bp_v[lower:upper, :])
        return (bt_v[lower:upper, :] << (pair_bits + 2)) | (swapped << 2) | (bs_v[lower:upper, :] + 1)

    codes = [pack(i * LANES, (i + 1) * LANES).astype(f32).T.astype(jnp.int32) for i in range(full)]
    for i, code in enumerate(codes):
        target = code >> (pair_bits + 2)
        owner_v[i * cols : (i + 1) * cols, :] = (target >> column_bits).astype(f32)
        lo_v[i * cols : (i + 1) * cols, :] = (target & (cols - 1)).astype(f32)
    if rem:
        target = bt_v[full * LANES :, :]
        owner_v[full * cols : full * cols + rem, :] = (target >> column_bits).astype(f32)
        lo_v[full * cols : full * cols + rem, :] = (target & (cols - 1)).astype(f32)
        tail = pack(full * LANES, slots).astype(f32)
        tail = jnp.concatenate([tail] * rows + [jnp.zeros((LANES - rows * rem, cols), f32)], axis=0)
        codes.append(tail.T.astype(jnp.int32))
    swapped = [(code >> 2) & ((1 << pair_bits) - 1) for code in codes]
    signs = [((code & 3) - 1).astype(f32) for code in codes]
    lanes = [index & (LANES - 1) for index in swapped]
    pieces = [index >> (LANES.bit_length() - 1) for index in swapped]

    lo_ids = lax.broadcasted_iota(jnp.int32, (cols, LANES), 0).astype(f32).astype(bf16)
    items = slots * cols // LANES

    @pl.loop(0, items // build_rows)
    def _(i):
        for r in range(build_rows):
            row = i * build_rows + r
            wanted = jnp.broadcast_to(lo_v[pl.ds(row, 1), :].astype(bf16), (cols, LANES))
            match = jnp.where(lo_ids == wanted, jnp.ones((), bf16), jnp.zeros((), bf16))
            hot[:, pl.ds(pl.multiple_of(row * LANES, LANES), LANES)] = match

    for copy in gathers:
        copy.wait()
    slab[me_a] = c_v[...]
    c = jnp.concatenate([slab[i] for i in range(na)], axis=0)
    c_top, c_rest = split(c)
    lhs = jnp.concatenate([c_top, c_rest, c_top], axis=0).T.astype(bf16)
    local, focks = [], []
    for a in range(rows):
        local.append(jnp.sum(weight[a * alphas : (a + 1) * alphas] * c, axis=0, keepdims=True))
        g_top, g_rest = split(g[a * alphas : (a + 1) * alphas])
        focks.append(dot(lhs, jnp.concatenate([g_top, g_top, g_rest], axis=0).astype(bf16)))
    if rem:
        lane_ids = lax.broadcasted_iota(jnp.int32, (cols, LANES), 1)
        tail = lane_pick(focks[0], lanes[full], pieces[full])
        for a in range(1, rows):
            tail = jnp.where(lane_ids < a * rem, tail, lane_pick(focks[a], lanes[full], pieces[full]))
        top, rest = split((tail * signs[full]).T)
        for a in range(rows):
            vals[a, full * cols : full * cols + rem, :] = top[a * rem : (a + 1) * rem]
            vals[rows + a, full * cols : full * cols + rem, :] = rest[a * rem : (a + 1) * rem]

    for i in range(full):
        for a in range(rows):
            top, rest = split(lane_pick(focks[a], lanes[i], pieces[i]) * signs[i])
            vals[a, i * cols : (i + 1) * cols, :] = top
            vals[rows + a, i * cols : (i + 1) * cols, :] = rest
    owner_ids = lax.broadcasted_iota(jnp.int32, (nb, LANES), 0).astype(f32)

    def step(i, total):
        lhs = []
        for r in range(step_rows):
            row = i * step_rows + r
            match = owner_ids == owner_v[pl.ds(row, 1), :]
            lhs.append(
                jnp.concatenate([jnp.where(match, vals[m, pl.ds(row, 1), :], 0.0) for m in range(2 * rows)], axis=0)
            )
        lhs = jnp.concatenate(lhs, axis=1).astype(bf16)
        width = step_rows * LANES
        return total + dot(hot[:, pl.ds(pl.multiple_of(i * width, LANES), width)], lhs, NT)

    total = lax.fori_loop(0, items // step_rows, step, jnp.zeros((cols, 2 * rows * nb), f32))
    if total.shape[1] % LANES:
        total = jnp.concatenate([total, jnp.zeros((cols, -total.shape[1] % LANES), f32)], axis=1)
    total = total.T
    for a in range(rows):
        send[:, a, :] = total[a * nb : (a + 1) * nb] + total[(rows + a) * nb : (rows + a + 1) * nb]

    copies = []
    for k in range(1, nb):
        to = lax.rem(me_b + k, nb)
        copy = pltpu.make_async_remote_copy(
            src_ref=send.at[to],
            dst_ref=recv.at[k - 1],
            send_sem=rs_send.at[k - 1],
            recv_sem=rs_recv.at[k - 1],
            device_id=(me_a, to),
            device_id_type=MESH,
        )
        copy.start()
        copies.append(copy)
    result = jnp.concatenate(local, axis=0) + send[me_b]
    for copy in copies:
        copy.wait()
    for k in range(1, nb):
        result = result + recv[k - 1]
    out[...] = result


def solution(mesh):
    na, nb = mesh.shape["alpha"], mesh.shape["beta"]

    def per_device(coeffs, a_target, a_pair, a_sign, b_target, b_pair, b_sign, integrals, one_body):
        rows, cols = coeffs.shape
        slots = a_target.shape[1]
        norb = one_body.shape[0]
        wide = pl.cdiv(norb * norb, LANES) * LANES
        items = slots * cols // LANES
        build_rows = next(n for n in range(44, 0, -1) if items % n == 0)
        step_rows = items
        i32, f32 = jnp.int32, jnp.float32
        padded = pl.cdiv(items, 8) * 8
        return pl.pallas_call(
            functools.partial(kernel, na, nb, build_rows, step_rows),
            out_shape=jax.ShapeDtypeStruct((rows, cols), f32),
            in_specs=[pl.BlockSpec(memory_space=pl.ANY)] * 9,
            out_specs=pl.BlockSpec(memory_space=pltpu.VMEM),
            scratch_shapes=[
                pltpu.VMEM(coeffs.shape, f32),
                pltpu.VMEM(a_target.shape, i32),
                pltpu.VMEM(a_pair.shape, i32),
                pltpu.VMEM(a_sign.shape, i32),
                pltpu.VMEM(b_target.shape[::-1], i32),
                pltpu.VMEM(b_pair.shape[::-1], i32),
                pltpu.VMEM(b_sign.shape[::-1], i32),
                pltpu.VMEM(integrals.shape, f32),
                pltpu.VMEM(one_body.shape, f32),
                pltpu.VMEM((na, rows, cols), f32),
                pltpu.VMEM((rows * na * rows, wide), f32),
                pltpu.VMEM((padded, LANES), f32),
                pltpu.VMEM((padded, LANES), f32),
                pltpu.VMEM((2 * rows, padded, LANES), f32),
                pltpu.VMEM((cols, items * LANES), jnp.bfloat16),
                pltpu.VMEM((nb, rows, cols), f32),
                pltpu.VMEM((nb - 1, rows, cols), f32),
                pltpu.SemaphoreType.DMA((9,)),
                pltpu.SemaphoreType.DMA((na - 1,)),
                pltpu.SemaphoreType.DMA((na - 1,)),
                pltpu.SemaphoreType.DMA((nb - 1,)),
                pltpu.SemaphoreType.DMA((nb - 1,)),
            ],
            compiler_params=pltpu.CompilerParams(collective_id=0, has_side_effects=True),
        )(coeffs, a_target, a_pair, a_sign, b_target.T, b_pair.T, b_sign.T, integrals, one_body)

    placed = (
        P("alpha", "beta"),
        P("alpha", None),
        P("alpha", None),
        P("alpha", None),
        P("beta", None),
        P("beta", None),
        P("beta", None),
        P(),
        P(),
    )
    return jax.shard_map(
        per_device, mesh=mesh, in_specs=placed, out_specs=P("alpha", "beta"), check_vma=False
    )
```
